512 devices in a mesh: row: 16 (over z, core), col: 32 (over x, y).
Axes of the slice: x: 4, y: 8, z: 8, core: 2. Of those that a mesh axis runs over, the one named last changes fastest.
Arguments:
- matrix: float32 [8192, 8192], P('row', 'col'), may hold values from -6 to 6
- inverses: float32 [4, 256, 256], P(None, 'row'), may hold values from -0.01171875 to 0.01171875
- pivots: int32 [4], replicated, may hold values from 0 to 31, as said below
- row_mask: int32 [4, 32], replicated, may hold values 0 or 1
- col_mask: int32 [4, 32], replicated, may hold values 0 or 1
Outputs:
- factored: float32 [8192, 8192], P('row', 'col')
The draws below stay inside these ranges and needn't reach their ends.
Inputs may be any that keep to these rules, and one draw needn't show every extreme that they name: `pivots`: 4 distinct block indices; 0 and 31 are always among them.
All inputs are finite; a program needn't handle non-finite values.
Results may differ from the reference program's by a relative error of at most 0.0001.
Values sent between devices are 32-bit elements; how exact they have to be, the bound alone decides.
A program may use at most 64 MiB of HBM per device.

```python
import jax
import jax.numpy as jnp
from jax import lax

B = 256
PANELS = 4
NB = 32
N = 8192


def draw_pivots(key, part):
    first_key = jax.random.fold_in(key, 11)
    second_key = jax.random.fold_in(key, 23)
    middle = jax.random.permutation(first_key, NB - 2) + 1
    chosen = jnp.concatenate([jnp.array([0, NB - 1], jnp.int32), middle[:PANELS - 2].astype(jnp.int32)])
    shuffle = jax.random.permutation(second_key, PANELS)
    return chosen[shuffle].astype(jnp.int32)


def set_ends(drawn, stream_key, least, top_value):
    spot = [jax.random.randint(jax.random.fold_in(stream_key, axis), (), 0, length) for axis, length in enumerate(drawn.shape)]
    longest = drawn.shape.index(max(drawn.shape))
    beside = spot[:longest] + [(spot[longest] + 1) % drawn.shape[longest]] + spot[longest + 1:]
    return drawn.at[tuple(spot)].set(least).at[tuple(beside)].set(top_value)


def block_levels(rng, extent, cuts, least, top_value):
    gain = 1.0
    for axis_at, parts in cuts:
        heights = jax.random.uniform(jax.random.fold_in(jax.random.fold_in(rng, 6), axis_at), (parts,), jnp.float32, least / len(cuts), top_value / len(cuts))
        gain = gain * jnp.repeat(jnp.exp(heights), extent[axis_at] // parts).reshape((-1,) + (1,) * (len(extent) - 1 - axis_at))
    return gain


def scatter_about(rng, shape, deviation, bound, pieces=(), kind=jnp.bfloat16):
    values = deviation * jax.random.normal(rng, shape, jnp.float32)
    if pieces:
        values = values * block_levels(rng, shape, pieces, -0.22, 0.18)
    return jnp.clip(values, -bound, bound).astype(kind)


def setup_inputs(seed: int = 0) -> dict:
    seeds = jax.random.split(jax.random.key(seed), 6)
    return {
        "matrix": scatter_about(seeds[0], (N, N), 1.0, 6.0, ((0, 16), (1, 32)), jnp.float32),
        "inverses": scatter_about(seeds[1], (PANELS, B, B), (4 * B * B) ** -0.5, 0.01171875, ((1, 16),), jnp.float32),
        "pivots": draw_pivots(jax.random.fold_in(seeds[5], 71), 0),
        "row_mask": set_ends((jax.random.randint(seeds[3], (PANELS, NB), 0, 4) < 3).astype(jnp.int32), jax.random.fold_in(seeds[3], 1), 0, 1),
        "col_mask": set_ends((jax.random.randint(seeds[4], (PANELS, NB), 0, 4) < 3).astype(jnp.int32), jax.random.fold_in(seeds[4], 1), 0, 1),
    }


def reference(matrix, inverses, pivots, row_mask, col_mask):
    highest = lax.Precision.HIGHEST
    block_ids = jnp.arange(NB, dtype=jnp.int32)
    current = matrix
    eliminated = jnp.zeros((NB,), jnp.float32)
    for step in range(PANELS):
        pivot_block = pivots[step]
        start = (pivot_block * B).astype(jnp.int32)
        anchor = jnp.zeros((), jnp.int32)
        row_block = lax.dynamic_slice(current, (start, anchor), (B, NB * B))
        solved = jnp.dot(inverses[step], row_block, precision=highest, preferred_element_type=jnp.float32)
        keep_cols = jnp.repeat(1.0 - eliminated, B)
        new_row = jnp.where(keep_cols[None, :] > 0.5, solved, row_block)
        current = lax.dynamic_update_slice(current, new_row, (start, anchor))
        eliminated = jnp.maximum(eliminated, (block_ids == pivot_block).astype(jnp.float32))
        living = 1.0 - eliminated
        row_factor = jnp.repeat(row_mask[step].astype(jnp.float32) * living, B)
        col_factor = jnp.repeat(col_mask[step].astype(jnp.float32) * living, B)
        panel_cols = lax.dynamic_slice(current, (anchor, start), (NB * B, B))
        left_part = panel_cols * row_factor[:, None]
        right_part = solved * col_factor[None, :]
        current = current - jnp.dot(left_part, right_part, precision=highest, preferred_element_type=jnp.float32)
    return current
```

```python
import functools

import jax
import jax.numpy as jnp
from jax import lax
from jax.experimental import pallas as pl
from jax.experimental.pallas import tpu as pltpu
from jax.sharding import PartitionSpec as P

MESH = pl.DeviceIdType.MESH
F32 = jnp.float32
BF16 = jnp.bfloat16


class Sems:
    def __init__(self, send, recv):
        self.send, self.recv, self.used = send, recv, 0

    def take(self, count=1):
        first = self.used
        self.used += count
        return first

    def copy(self, src, dst, device, index):
        return pltpu.make_async_remote_copy(
            src_ref=src,
            dst_ref=dst,
            send_sem=self.send.at[index],
            recv_sem=self.recv.at[index],
            device_id=device,
            device_id_type=MESH,
        )


class Ring:
    def __init__(self, sems, n, me, view, right, left, first=None):
        self.n, self.steps = n, n // 2
        self.down, self.up = [], []
        for s in range(self.steps):
            slot = lax.rem(me - s + n, n)
            src = first if s == 0 and first is not None else view(slot)
            self.down.append(sems.copy(src, view(slot), right, sems.take()))
            if s < n - 1 - self.steps:
                slot = lax.rem(me + s, n)
                src = first if s == 0 and first is not None else view(slot)
                self.up.append(sems.copy(src, view(slot), left, sems.take()))

    def start(self, s):
        for way in (self.down, self.up):
            if s < len(way):
                way[s].start()

    def arrive(self, s):
        for way in (self.down, self.up):
            if s < len(way):
                way[s].wait_recv()

    def go(self, s):
        if s > 0:
            self.arrive(s - 1)
        if s < self.steps:
            self.start(s)

    def drain(self):
        for way in (self.down, self.up):
            for copy in way:
                copy.wait_send()


def gather_kernel(
    nz, nx, ny, panels, pivots, a, inv, colg, ppg, rowg, invg,
    recv_c, recv_r, zbuf, xbuf, send_a, recv_a, send_b, recv_b, send_s, recv_s,
):
    rows, cols = 2 * nz, nx * ny
    half = panels // 2
    r, c = lax.axis_index("row"), lax.axis_index("col")
    z, core = r // 2, lax.rem(r, 2)
    x, y = c // ny, lax.rem(c, ny)

    barrier = pltpu.get_barrier_semaphore()

    def greet_col(d, carry):
        peer = lax.rem(c + d, cols)
        pl.semaphore_signal(barrier, inc=1, device_id={"col": peer}, device_id_type=MESH)
        return carry

    def greet_row(d, carry):
        peer = lax.rem(r + d, rows)
        pl.semaphore_signal(barrier, inc=1, device_id={"row": peer}, device_id_type=MESH)
        return carry

    lax.fori_loop(1, cols, greet_col, 0)
    lax.fori_loop(1, rows, greet_row, 0)
    pl.semaphore_wait(barrier, cols + rows - 2)

    sems = Sems(send_s, recv_s)

    def to_col(d):
        peer = lax.rem(c + d, cols)
        return pltpu.make_async_remote_copy(
            src_ref=a.at[:, peer], dst_ref=recv_c.at[c],
            send_sem=send_a.at[d], recv_sem=recv_a.at[d],
            device_id={"col": peer}, device_id_type=MESH,
        )

    def to_row(d):
        peer = lax.rem(r + d, rows)
        return pltpu.make_async_remote_copy(
            src_ref=a.at[:, pl.ds(2 * peer, 2)], dst_ref=recv_r.at[r],
            send_sem=send_b.at[d], recv_sem=recv_b.at[d],
            device_id={"row": peer}, device_id_type=MESH,
        )

    def loop(low, high, act):
        def body(d, carry):
            act(d)
            return carry
        lax.fori_loop(low, high, body, 0)

    loop(1, cols, lambda d: to_col(d).start())
    loop(1, rows, lambda d: to_row(d).start())

    y_right = {"col": x * ny + lax.rem(y + 1, ny)}
    y_left = {"col": x * ny + lax.rem(y + ny - 1, ny)}
    z_right = {"row": 2 * lax.rem(z + 1, nz) + core}
    z_left = {"row": 2 * lax.rem(z + nz - 1, nz) + core}
    partner = {"row": 2 * z + 1 - core}

    def ring_y(view):
        return Ring(sems, ny, y, view, y_right, y_left)

    def ring_z(view, first=None):
        return Ring(sems, nz, z, view, z_right, z_left, first)

    def spread_x(ref):
        copies = []
        for d in range(1, nx):
            peer = lax.rem(x + d, nx)
            copies.append(sems.copy(ref, ref, {"col": peer * ny + y}, sems.take()))
        return copies

    def start(copies):
        for copy in copies:
            copy.start()

    def to_partner(ref):
        return sems.copy(ref, ref, partner, sems.take())

    ring_inv = ring_z(lambda i: invg.at[i, core], inv)
    ring_inv.start(0)
    invg[z, core] = inv[...]
    recv_c[c] = a[:, c]
    recv_r[r] = a[:, pl.ds(2 * r, 2)]

    loop(1, cols, lambda d: to_col(d).wait_recv())
    for h in range(half):
        theirs = recv_c[pivots[(1 - core) * half + h]]
        for b in range(2):
            xbuf[b, h] = theirs[b]
    for m in range(panels):
        piece = recv_c[pivots[m]]
        for b in range(2):
            colg[b, x, y, m] = piece[b]
    for h in range(half):
        mine = recv_c[pivots[core * half + h]]
        for b in range(2):
            zbuf[z, 2 * core + b, h] = mine[b]

    swap = sems.copy(xbuf, zbuf.at[z, pl.ds(2 * core, 2)], partner, sems.take())
    swap.start()
    col0_x = spread_x(colg.at[0, x, y])
    start(col0_x)
    col1 = ring_y(lambda i: colg.at[1, x, i])
    col1.start(0)
    swap.wait_recv()
    ppz = ring_z(lambda i: zbuf.at[i])
    ppz.start(0)
    for copy in col0_x:
        copy.wait_recv()
    col0 = ring_y(lambda i: colg.at[0, :, i])
    col0.start(0)

    for s in range(1, max(nz // 2, ny // 2)):
        if s < nz // 2:
            ppz.go(s)
        if s < ny // 2:
            col1.go(s)
            if s > 1:
                col0.go(s - 1)
        if s < nz // 2:
            ring_inv.go(s)

    ppz.arrive(nz // 2 - 1)
    for h in range(half):
        m = core * half + h
        for j in range(panels - 1):
            k = j + (j >= m).astype(jnp.int32)
            p = pivots[k]
            ppg[m, x, y, j] = zbuf[p // 4, lax.rem(p, 4), h]
    m0, m1 = core * half, core * half + 1
    pp0_x = spread_x(ppg.at[m0, x, y])
    start(pp0_x)
    pp1 = ring_y(lambda i: ppg.at[m1, x, i])
    pp1.start(0)
    col1.arrive(ny // 2 - 1)
    col1_x = spread_x(colg.at[1, x])
    start(col1_x)
    col0.go(ny // 2 - 1)
    ring_inv.arrive(nz // 2 - 1)
    inv_swap = to_partner(invg.at[:, core])
    inv_swap.start()

    loop(1, rows, lambda d: to_row(d).wait_recv())
    for k in range(panels):
        p = pivots[k]
        rowg[z, core, k] = recv_r[p // 2, lax.rem(p, 2)]
    ring_row = ring_z(lambda i: rowg.at[i, core])
    ring_row.start(0)

    pp0 = ring_y(lambda i: ppg.at[m0, :, i])
    forwards = []

    def forward(ref):
        copy = to_partner(ref)
        copy.start()
        forwards.append(copy)

    for copy in pp0_x:
        copy.wait_recv()
    pp0.start(0)
    forward(ppg.at[m0, :, y])
    for s in range(1, max(nz // 2, ny // 2)):
        if s < ny // 2:
            pp1.go(s)
            if s > 1:
                pp0.go(s - 1)
                forward(ppg.at[m0, :, lax.rem(y - s + 1 + ny, ny)])
                forward(ppg.at[m0, :, lax.rem(y + s - 1, ny)])
        if s < nz // 2:
            ring_row.go(s)
    pp1.arrive(ny // 2 - 1)
    pp1_x = spread_x(ppg.at[m1, x])
    start(pp1_x)
    forward(ppg.at[m1, x])
    last = ny // 2 - 1
    if last > 0:
        pp0.go(last)
        forward(ppg.at[m0, :, lax.rem(y - last + ny, ny)])
        forward(ppg.at[m0, :, lax.rem(y + last, ny)])
    ring_row.arrive(nz // 2 - 1)
    row_swap = to_partner(rowg.at[:, core])
    row_swap.start()
    pp0.arrive(last)
    forward(ppg.at[m0, :, lax.rem(y + ny // 2, ny)])
    for d, copy in enumerate(pp1_x):
        copy.wait_recv()
        forward(ppg.at[m1, lax.rem(x - d - 1 + nx, nx)])
    col0.arrive(last)
    for copy in col1_x:
        copy.wait_recv()
    inv_swap.wait_recv()
    row_swap.wait_recv()
    for copy in forwards:
        copy.wait_recv()

    for ring in (ring_inv, ppz, col0, col1, pp0, pp1, ring_row):
        ring.drain()
    for copy in [swap, inv_swap, row_swap] + col0_x + col1_x + pp0_x + pp1_x + forwards:
        copy.wait_send()
    loop(1, cols, lambda d: to_col(d).wait_send())
    loop(1, rows, lambda d: to_row(d).wait_send())


def halves(value):
    high = value.astype(BF16)
    return high, (value - high.astype(F32)).astype(BF16)


def product(left, right):
    (lh, ll), (rh, rl) = left, right
    dot = functools.partial(jnp.dot, preferred_element_type=F32)
    return dot(lh, rh) + (dot(lh, rl) + dot(ll, rh))


def local_kernel(panels, width, place, pivots, row_mask, col_mask, a, colg, ppg, rowg, invg, out, work, xh, xl, keep):
    own = panels
    my_col = place[1]
    my_rows = [place[0] * 2 + b for b in range(2)]
    square = (width, width)

    for b in range(2):
        work[b, own] = a[b].reshape(square)
        for m in range(panels):
            work[b, m] = colg[b, :, :, m].reshape(square)
    for k in range(panels):
        work[2 + k, own] = rowg[:, :, k].reshape(square)
        for m in range(panels):
            if m != k:
                work[2 + k, m] = ppg[m, :, :, k - (k > m)].reshape(square)

    def done(block, step):
        hit = block == pivots[0]
        for k in range(1, step + 1):
            hit = hit | (block == pivots[k])
        return hit

    for step in range(panels):
        inverse = halves(invg[:, :, step].reshape(square))
        factors = [
            jnp.where(done(i, step), 0.0, row_mask[step, i].astype(F32)) for i in my_rows
        ] + [row_mask[step, pivots[k]].astype(F32) for k in range(step + 1, panels)]
        places = [0, 1] + [2 + k for k in range(step + 1, panels)]
        for n, (i, factor) in enumerate(zip(places, factors)):
            high, low = halves(work[i, step] * factor)
            xh[pl.ds(n * width, width), :] = high
            xl[pl.ds(n * width, width), :] = low
        my_factor = jnp.where(done(my_col, step), 0.0, col_mask[step, my_col].astype(F32))

        def column(j, carry):
            solved = product(inverse, halves(work[2 + step, j]))
            mine = j == own
            factor = jnp.where(
                mine, my_factor, col_mask[step, pivots[jnp.minimum(j, panels - 1)]].astype(F32)
            )

            @pl.when(mine)
            def _():
                keep[step] = solved

            right = halves(solved * factor)
            for n, i in enumerate(places):
                span = pl.ds(n * width, width)
                work[i, j] -= product((xh[span, :], xl[span, :]), right)
            return carry

        lax.fori_loop(step + 1, panels + 1, column, 0)

    for b in range(2):
        out[pl.ds(b * width, width), :] = work[b, own]
        for k in range(panels):
            mine = my_rows[b] == pivots[k]

            if k == 0:
                @pl.when(mine)
                def _():
                    out[pl.ds(b * width, width), :] = keep[0]
            else:
                gone = done(my_col, k - 1)

                @pl.when(mine & gone)
                def _():
                    out[pl.ds(b * width, width), :] = work[2 + k, own]

                @pl.when(mine & jnp.logical_not(gone))
                def _():
                    out[pl.ds(b * width, width), :] = keep[k]


def on_device(nz, nx, ny, matrix, inverses, pivots, row_mask, col_mask):
    panels, _, width = inverses.shape
    rows, cols = 2 * nz, nx * ny
    part = width // cols
    blocks = matrix.reshape(2, cols, part, width)
    slices = inverses.reshape(panels, 2, part, width)
    vmem = pl.BlockSpec(memory_space=pltpu.VMEM)
    smem = pl.BlockSpec(memory_space=pltpu.SMEM)
    half = panels // 2
    count = 256
    gathered = pl.pallas_call(
        functools.partial(gather_kernel, nz, nx, ny, panels),
        out_shape=(
            jax.ShapeDtypeStruct((2, nx, ny, panels, part, width), F32),
            jax.ShapeDtypeStruct((panels, nx, ny, panels - 1, part, width), F32),
            jax.ShapeDtypeStruct((nz, 2, panels, 2, part, width), F32),
            jax.ShapeDtypeStruct((nz, 2, panels, 2, part, width), F32),
        ),
        in_specs=[smem, vmem, vmem],
        out_specs=(vmem,) * 4,
        scratch_shapes=[
            pltpu.VMEM((cols, 2, part, width), F32),
            pltpu.VMEM((rows, 2, 2, part, width), F32),
            pltpu.VMEM((nz, 4, half, part, width), F32),
            pltpu.VMEM((2, half, part, width), F32),
            pltpu.SemaphoreType.DMA((cols,)),
            pltpu.SemaphoreType.DMA((cols,)),
            pltpu.SemaphoreType.DMA((rows,)),
            pltpu.SemaphoreType.DMA((rows,)),
            pltpu.SemaphoreType.DMA((count,)),
            pltpu.SemaphoreType.DMA((count,)),
        ],
        compiler_params=pltpu.CompilerParams(collective_id=0, has_side_effects=True),
        name="gather",
    )(pivots, blocks, slices)
    place = jnp.stack([lax.axis_index("row"), lax.axis_index("col")]).astype(jnp.int32)
    return pl.pallas_call(
        functools.partial(local_kernel, panels, width),
        out_shape=jax.ShapeDtypeStruct((2 * width, width), F32),
        in_specs=[smem] * 4 + [vmem] * 5,
        out_specs=vmem,
        scratch_shapes=[
            pltpu.VMEM((2 + panels, 1 + panels, width, width), F32),
            pltpu.VMEM(((1 + panels) * width, width), BF16),
            pltpu.VMEM(((1 + panels) * width, width), BF16),
            pltpu.VMEM((panels, width, width), F32),
        ],
        name="eliminate",
    )(place, pivots, row_mask, col_mask, blocks, *gathered)


def solution(mesh):
    rows, cols = mesh.shape["row"], mesh.shape["col"]
    nx = 4 if cols == 32 else 2
    in_specs = (P("row", "col"), P(None, "row", None), P(), P(), P())
    return jax.shard_map(
        functools.partial(on_device, rows // 2, nx, cols // nx),
        mesh=mesh, in_specs=in_specs, out_specs=P("row", "col"), check_vma=False,
    )
```

```python
import functools

import jax
import jax.numpy as jnp
from jax import lax
from jax.experimental import pallas as pl
from jax.experimental.pallas import tpu as pltpu
from jax.sharding import PartitionSpec as P

MESH = pl.DeviceIdType.MESH
F32 = jnp.float32
BF16 = jnp.bfloat16


class Sems:
    def __init__(self, send, recv):
        self.send, self.recv, self.used = send, recv, 0

    def take(self, count=1):
        first = self.used
        self.used += count
        return first

    def copy(self, src, dst, device, index):
        return pltpu.make_async_remote_copy(
            src_ref=src,
            dst_ref=dst,
            send_sem=self.send.at[index],
            recv_sem=self.recv.at[index],
            device_id=device,
            device_id_type=MESH,
        )


class Ring:
    def __init__(self, sems, n, me, view, right, left, first=None):
        self.n, self.steps = n, n // 2
        self.down, self.up = [], []
        for s in range(self.steps):
            slot = lax.rem(me - s + n, n)
            src = first if s == 0 and first is not None else view(slot)
            self.down.append(sems.copy(src, view(slot), right, sems.take()))
            if s < n - 1 - self.steps:
                slot = lax.rem(me + s, n)
                src = first if s == 0 and first is not None else view(slot)
                self.up.append(sems.copy(src, view(slot), left, sems.take()))

    def start(self, s):
        for way in (self.down, self.up):
            if s < len(way):
                way[s].start()

    def arrive(self, s):
        for way in (self.down, self.up):
            if s < len(way):
                way[s].wait_recv()

    def go(self, s):
        if s > 0:
            self.arrive(s - 1)
        if s < self.steps:
            self.start(s)

    def drain(self):
        for way in (self.down, self.up):
            for copy in way:
                copy.wait_send()


def gather(
    nz, nx, ny, panels, pivots, a, inv, colg, ppg, rowg, invg,
    recv_c, recv_r, zbuf, xbuf, send_a, recv_a, send_b, recv_b, send_s, recv_s,
):
    rows, cols = 2 * nz, nx * ny
    half = panels // 2
    r, c = lax.axis_index("row"), lax.axis_index("col")
    z, core = r // 2, lax.rem(r, 2)
    x, y = c // ny, lax.rem(c, ny)

    barrier = pltpu.get_barrier_semaphore()

    def greet_col(d, carry):
        peer = lax.rem(c + d, cols)
        pl.semaphore_signal(barrier, inc=1, device_id={"col": peer}, device_id_type=MESH)
        return carry

    def greet_row(d, carry):
        peer = lax.rem(r + d, rows)
        pl.semaphore_signal(barrier, inc=1, device_id={"row": peer}, device_id_type=MESH)
        return carry

    lax.fori_loop(1, cols, greet_col, 0)
    lax.fori_loop(1, rows, greet_row, 0)
    pl.semaphore_wait(barrier, cols + rows - 2)

    sems = Sems(send_s, recv_s)

    def to_col(d):
        peer = lax.rem(c + d, cols)
        return pltpu.make_async_remote_copy(
            src_ref=a.at[:, peer], dst_ref=recv_c.at[c],
            send_sem=send_a.at[d], recv_sem=recv_a.at[d],
            device_id={"col": peer}, device_id_type=MESH,
        )

    def to_row(d):
        peer = lax.rem(r + d, rows)
        return pltpu.make_async_remote_copy(
            src_ref=a.at[:, pl.ds(2 * peer, 2)], dst_ref=recv_r.at[r],
            send_sem=send_b.at[d], recv_sem=recv_b.at[d],
            device_id={"row": peer}, device_id_type=MESH,
        )

    def loop(low, high, act):
        def body(d, carry):
            act(d)
            return carry
        lax.fori_loop(low, high, body, 0)

    loop(1, cols, lambda d: to_col(d).start())
    loop(1, rows, lambda d: to_row(d).start())

    y_right = {"col": x * ny + lax.rem(y + 1, ny)}
    y_left = {"col": x * ny + lax.rem(y + ny - 1, ny)}
    z_right = {"row": 2 * lax.rem(z + 1, nz) + core}
    z_left = {"row": 2 * lax.rem(z + nz - 1, nz) + core}
    partner = {"row": 2 * z + 1 - core}

    def ring_y(view):
        return Ring(sems, ny, y, view, y_right, y_left)

    def ring_z(view, first=None):
        return Ring(sems, nz, z, view, z_right, z_left, first)

    def spread_x(ref):
        copies = []
        for d in range(1, nx):
            peer = lax.rem(x + d, nx)
            copies.append(sems.copy(ref, ref, {"col": peer * ny + y}, sems.take()))
        return copies

    def start(copies):
        for copy in copies:
            copy.start()

    def to_partner(ref):
        return sems.copy(ref, ref, partner, sems.take())

    ring_inv = ring_z(lambda i: invg.at[i, core], inv)
    ring_inv.start(0)
    invg[z, core] = inv[...]
    recv_c[c] = a[:, c]
    recv_r[r] = a[:, pl.ds(2 * r, 2)]

    loop(1, cols, lambda d: to_col(d).wait_recv())
    for h in range(half):
        theirs = recv_c[pivots[(1 - core) * half + h]]
        for b in range(2):
            xbuf[b, h] = theirs[b]
    for m in range(panels):
        piece = recv_c[pivots[m]]
        for b in range(2):
            colg[b, x, y, m] = piece[b]
    for h in range(half):
        mine = recv_c[pivots[core * half + h]]
        for b in range(2):
            zbuf[z, 2 * core + b, h] = mine[b]

    swap = sems.copy(xbuf, zbuf.at[z, pl.ds(2 * core, 2)], partner, sems.take())
    swap.start()
    col0_x = spread_x(colg.at[0, x, y])
    start(col0_x)
    col1 = ring_y(lambda i: colg.at[1, x, i])
    col1.start(0)
    swap.wait_recv()
    ppz = ring_z(lambda i: zbuf.at[i])
    ppz.start(0)
    for copy in col0_x:
        copy.wait_recv()
    col0 = ring_y(lambda i: colg.at[0, :, i])
    col0.start(0)

    for s in range(1, max(nz // 2, ny // 2)):
        if s < nz // 2:
            ppz.go(s)
        if s < ny // 2:
            col1.go(s)
            if s > 1:
                col0.go(s - 1)
        if s < nz // 2:
            ring_inv.go(s)

    ppz.arrive(nz // 2 - 1)
    for h in range(half):
        m = core * half + h
        for j in range(panels - 1):
            k = j + (j >= m).astype(jnp.int32)
            p = pivots[k]
            ppg[m, x, y, j] = zbuf[p // 4, lax.rem(p, 4), h]
    m0, m1 = core * half, core * half + 1
    pp0_x = spread_x(ppg.at[m0, x, y])
    start(pp0_x)
    pp1 = ring_y(lambda i: ppg.at[m1, x, i])
    pp1.start(0)
    col1.arrive(ny // 2 - 1)
    col1_x = spread_x(colg.at[1, x])
    start(col1_x)
    col0.go(ny // 2 - 1)
    ring_inv.arrive(nz // 2 - 1)
    inv_swap = to_partner(invg.at[:, core])
    inv_swap.start()

    loop(1, rows, lambda d: to_row(d).wait_recv())
    for k in range(panels):
        p = pivots[k]
        rowg[z, core, k] = recv_r[p // 2, lax.rem(p, 2)]
    ring_row = ring_z(lambda i: rowg.at[i, core])
    ring_row.start(0)

    pp0 = ring_y(lambda i: ppg.at[m0, :, i])
    forwards = []

    def forward(ref):
        copy = to_partner(ref)
        copy.start()
        forwards.append(copy)

    for copy in pp0_x:
        copy.wait_recv()
    pp0.start(0)
    forward(ppg.at[m0, :, y])
    for s in range(1, max(nz // 2, ny // 2)):
        if s < ny // 2:
            pp1.go(s)
            if s > 1:
                pp0.go(s - 1)
                forward(ppg.at[m0, :, lax.rem(y - s + 1 + ny, ny)])
                forward(ppg.at[m0, :, lax.rem(y + s - 1, ny)])
        if s < nz // 2:
            ring_row.go(s)
    pp1.arrive(ny // 2 - 1)
    pp1_x = spread_x(ppg.at[m1, x])
    start(pp1_x)
    forward(ppg.at[m1, x])
    last = ny // 2 - 1
    if last > 0:
        pp0.go(last)
        forward(ppg.at[m0, :, lax.rem(y - last + ny, ny)])
        forward(ppg.at[m0, :, lax.rem(y + last, ny)])
    ring_row.arrive(nz // 2 - 1)
    row_swap = to_partner(rowg.at[:, core])
    row_swap.start()
    pp0.arrive(last)
    forward(ppg.at[m0, :, lax.rem(y + ny // 2, ny)])
    for d, copy in enumerate(pp1_x):
        copy.wait_recv()
        forward(ppg.at[m1, lax.rem(x - d - 1 + nx, nx)])
    col0.arrive(last)
    for copy in col1_x:
        copy.wait_recv()
    inv_swap.wait_recv()
    row_swap.wait_recv()
    for copy in forwards:
        copy.wait_recv()

    for ring in (ring_inv, ppz, col0, col1, pp0, pp1, ring_row):
        ring.drain()
    for copy in [swap, inv_swap, row_swap] + col0_x + col1_x + pp0_x + pp1_x + forwards:
        copy.wait_send()
    loop(1, cols, lambda d: to_col(d).wait_send())
    loop(1, rows, lambda d: to_row(d).wait_send())


def halves(value):
    high = value.astype(BF16)
    return high, (value - high.astype(F32)).astype(BF16)


def product(left, right):
    (lh, ll), (rh, rl) = left, right
    dot = functools.partial(jnp.dot, preferred_element_type=F32)
    return dot(lh, rh) + (dot(lh, rl) + dot(ll, rh))


def eliminate(panels, width, pivots, row_mask, col_mask, a, colg, ppg, rowg, invg, out, xh, xl, keep):
    my_col = lax.axis_index("col")
    my_rows = [lax.axis_index("row") * 2 + b for b in range(2)]
    square = (width, width)

    def whole(ref, *index):
        return ref[index].reshape(square)

    def left_of(i, step):
        if i < 2:
            return whole(colg, i, slice(None), slice(None), step)
        return whole(ppg, step, slice(None), slice(None), i - 2 - (i - 2 > step))

    def done(block, step):
        hit = block == pivots[0]
        for k in range(1, step + 1):
            hit = hit | (block == pivots[k])
        return hit

    for step in range(panels):
        inverse = halves(whole(invg, slice(None), slice(None), step))
        later = range(step + 1, panels)
        factors = [jnp.where(done(i, step), 0.0, row_mask[step, i].astype(F32)) for i in my_rows]
        factors += [row_mask[step, pivots[k]].astype(F32) for k in later]
        places = [0, 1] + [2 + k for k in later]
        for n, (i, factor) in enumerate(zip(places, factors)):
            high, low = halves(left_of(i, step) * factor)
            xh[n] = high
            xl[n] = low
        for j in later:
            solved = product(inverse, halves(left_of(2 + step, j)))
            right = halves(solved * col_mask[step, pivots[j]].astype(F32))
            for n, i in enumerate(places):
                if i - 2 == j:
                    continue
                change = product((xh[n], xl[n]), right)
                if i < 2:
                    shape = colg.shape[1:3] + colg.shape[4:]
                    colg[i, :, :, j] -= change.reshape(shape)
                else:
                    shape = ppg.shape[1:3] + ppg.shape[4:]
                    ppg[j, :, :, i - 2 - (i - 2 > j)] -= change.reshape(shape)
        solved = product(inverse, halves(whole(rowg, slice(None), slice(None), step)))
        keep[step] = solved
        factor = jnp.where(done(my_col, step), 0.0, col_mask[step, my_col].astype(F32))
        right = halves(solved * factor)
        for n, i in enumerate(places):
            change = product((xh[n], xl[n]), right)
            if i < 2:
                span = pl.ds(i * width, width)
                before = whole(a, i) if step == 0 else out[span, :]
                out[span, :] = before - change
            else:
                shape = rowg.shape[:2] + rowg.shape[3:]
                rowg[:, :, i - 2] -= change.reshape(shape)

    for b in range(2):
        span = pl.ds(b * width, width)
        value = out[span, :]
        for k in range(panels):
            mine = my_rows[b] == pivots[k]
            if k == 0:
                pivot_row = keep[k]
            else:
                pivot_row = jnp.where(done(my_col, k - 1), whole(rowg, slice(None), slice(None), k), keep[k])
            value = jnp.where(mine, pivot_row, value)
        out[span, :] = value


def on_device(nz, nx, ny, matrix, inverses, pivots, row_mask, col_mask):
    panels, _, width = inverses.shape
    rows, cols = 2 * nz, nx * ny
    part = width // cols
    blocks = matrix.reshape(2, cols, part, width)
    slices = inverses.reshape(panels, 2, part, width)
    vmem = pl.BlockSpec(memory_space=pltpu.VMEM)
    smem = pl.BlockSpec(memory_space=pltpu.SMEM)
    half = panels // 2
    count = 256
    return pl.pallas_call(
        functools.partial(kernel, nz, nx, ny, panels, width),
        out_shape=jax.ShapeDtypeStruct((2 * width, width), F32),
        in_specs=[smem, smem, smem, vmem, vmem],
        out_specs=vmem,
        scratch_shapes=[
            pltpu.VMEM((2, nx, ny, panels, part, width), F32),
            pltpu.VMEM((panels, nx, ny, panels - 1, part, width), F32),
            pltpu.VMEM((nz, 2, panels, 2, part, width), F32),
            pltpu.VMEM((nz, 2, panels, 2, part, width), F32),
            pltpu.VMEM((1 + panels, width, width), BF16),
            pltpu.VMEM((1 + panels, width, width), BF16),
            pltpu.VMEM((panels, width, width), F32),
            pltpu.VMEM((cols, 2, part, width), F32),
            pltpu.VMEM((rows, 2, 2, part, width), F32),
            pltpu.VMEM((nz, 4, half, part, width), F32),
            pltpu.VMEM((2, half, part, width), F32),
            pltpu.SemaphoreType.DMA((cols,)),
            pltpu.SemaphoreType.DMA((cols,)),
            pltpu.SemaphoreType.DMA((rows,)),
            pltpu.SemaphoreType.DMA((rows,)),
            pltpu.SemaphoreType.DMA((count,)),
            pltpu.SemaphoreType.DMA((count,)),
        ],
        compiler_params=pltpu.CompilerParams(collective_id=0, has_side_effects=True),
    )(pivots, row_mask, col_mask, blocks, slices)


def kernel(
    nz, nx, ny, panels, width, pivots, row_mask, col_mask, a, inv, out,
    colg, ppg, rowg, invg, xh, xl, keep, *scratch,
):
    gather(nz, nx, ny, panels, pivots, a, inv, colg, ppg, rowg, invg, *scratch)
    eliminate(panels, width, pivots, row_mask, col_mask, a, colg, ppg, rowg, invg, out, xh, xl, keep)


def solution(mesh):
    rows, cols = mesh.shape["row"], mesh.shape["col"]
    nx = 4 if cols == 32 else 2
    in_specs = (P("row", "col"), P(None, "row", None), P(), P(), P())
    return jax.shard_map(
        functools.partial(on_device, rows // 2, nx, cols // nx),
        mesh=mesh, in_specs=in_specs, out_specs=P("row", "col"), check_vma=False,
    )
```

```python
import functools

import jax
import jax.numpy as jnp
from jax import lax
from jax.experimental import pallas as pl
from jax.experimental.pallas import tpu as pltpu
from jax.sharding import PartitionSpec as P

MESH = pl.DeviceIdType.MESH
F32 = jnp.float32
BF16 = jnp.bfloat16
CHUNKS = 1
TIMES = {
    "a2a": (10.0,), "rows": 24.0, "swap": 2.5, "z": 5.0, "inv": 8.0, "row": 8.0, "share": 3.0,
    "col": ((5.0, 4.5), (5.0, 1.2)), "pp": ((3.5, 6.0), (4.0, 0.6)),
}


class Sems:
    def __init__(self, send, recv):
        self.send, self.recv, self.used = send, recv, 0

    def take(self, count=1):
        first = self.used
        self.used += count
        return first

    def copy(self, src, dst, device, index):
        return pltpu.make_async_remote_copy(
            src_ref=src,
            dst_ref=dst,
            send_sem=self.send.at[index],
            recv_sem=self.recv.at[index],
            device_id=device,
            device_id_type=MESH,
        )


class Ring:
    def __init__(self, sems, n, me, views, right, left):
        self.n, self.me, self.steps = n, me, n // 2
        self.pieces = []
        for view in views:
            ways = []
            for s in range(self.steps):
                slot = lax.rem(me - s + n, n)
                ways.append([sems.copy(view(slot), view(slot), right, sems.take())])
                if s < n - 1 - self.steps:
                    slot = lax.rem(me + s, n)
                    ways[-1].append(sems.copy(view(slot), view(slot), left, sems.take()))
            self.pieces.append(ways)

    def run(self, delay, arrived=None):
        for s in range(self.steps + 1):
            for n, ways in enumerate(self.pieces):
                if s > 0:
                    yield 0.3 if n else delay
                    for copy in ways[s - 1]:
                        copy.wait_recv()
                if s < self.steps:
                    for copy in ways[s]:
                        copy.start()
            if s > 0 and arrived is not None:
                arrived(lax.rem(self.me - s + self.n, self.n))
                if s < self.n - self.steps:
                    arrived(lax.rem(self.me + s, self.n))

    def drain(self):
        for ways in self.pieces:
            for step in ways:
                for copy in step:
                    copy.wait_send()


class Hops:
    def __init__(self, sems, n, me, views, at):
        self.n, self.me, self.all = n, me, []
        self.first, self.second = [], []

        def copy(view, slot, to):
            slot = lax.rem(me + slot + n, n)
            made = sems.copy(view(slot), view(slot), at(lax.rem(me + to + n, n)), sems.take())
            self.all.append(made)
            return made

        for p, view in enumerate(views):
            if n < 6:
                self.first.append([copy(view, 0, d) for d in range(1, n)])
                self.second.append([])
            else:
                self.first.append([copy(view, 0, d) for d in (2, -2, 1, -1)])
                far = 2 if p % 2 == 0 else -2
                self.second.append([copy(view, -2, 1), copy(view, 2, -1), copy(view, -far, far)])

    def slot(self, d):
        return lax.rem(self.me + d + self.n, self.n)

    def run(self, delay, arrived=None):
        for copies in self.first:
            for copy in copies:
                copy.start()
        for n, copies in enumerate(self.first):
            yield 0.3 if n else delay
            for copy in copies[:2]:
                copy.wait_recv()
            for copy in self.second[n]:
                copy.start()
        for copies in self.first:
            for copy in copies[2:]:
                copy.wait_recv()
        near = [-d for d in range(1, self.n)] if self.n < 6 else [-1, 1, -2, 2]
        if arrived is not None:
            for d in near:
                arrived(self.slot(d))
        if self.n >= 6:
            for n, copies in enumerate(self.second):
                yield 0.3 if n else delay
                for copy in copies:
                    copy.wait_recv()
            if arrived is not None:
                for d in (-3, 3, 4):
                    arrived(self.slot(d))

    def drain(self):
        for copy in self.all:
            copy.wait_send()


def interleave(chains):
    queue = [(start, n, chain) for n, (start, chain) in enumerate(chains)]
    count = len(queue)
    while queue:
        now, n, chain = min(queue, key=lambda item: item[:2])
        queue.remove((now, n, chain))
        for event in chain:
            if isinstance(event, tuple):
                queue.append((now + event[0], count, event[1]))
                count += 1
            else:
                queue.append((now + event, n, chain))
                break


def gather(
    nz, nx, ny, panels, pivots, a, inv, colg, ppg, rowg, invg,
    recv_c, recv_r, zbuf, xbuf, send_a, recv_a, send_b, recv_b, send_s, recv_s,
):
    rows, cols = 2 * nz, nx * ny
    half = panels // 2
    r, c = lax.axis_index("row"), lax.axis_index("col")
    z, core = r // 2, lax.rem(r, 2)
    x, y = c // ny, lax.rem(c, ny)
    lanes = colg.shape[-1] // CHUNKS

    barrier = pltpu.get_barrier_semaphore()

    def loop(low, high, act):
        def body(d, carry):
            act(d)
            return carry
        lax.fori_loop(low, high, body, 0)

    def greet(axis, me, n):
        loop(1, n, lambda d: pl.semaphore_signal(
            barrier, inc=1, device_id={axis: lax.rem(me + d, n)}, device_id_type=MESH
        ))

    greet("col", c, cols)
    greet("row", r, rows)
    recv_c[c] = a[:, c]
    recv_r[r] = a[:, pl.ds(2 * r, 2)]
    invg[z, core] = inv[...]
    pl.semaphore_wait(barrier, cols + rows - 2)

    sems = Sems(send_s, recv_s)

    def span(part):
        return pl.ds(part * lanes, lanes)

    def to_col(part, d):
        peer = lax.rem(c + d, cols)
        return pltpu.make_async_remote_copy(
            src_ref=a.at[:, peer, :, span(part)], dst_ref=recv_c.at[c, :, :, span(part)],
            send_sem=send_a.at[part, d], recv_sem=recv_a.at[part, d],
            device_id={"col": peer}, device_id_type=MESH,
        )

    def to_row(d):
        peer = lax.rem(r + d, rows)
        return pltpu.make_async_remote_copy(
            src_ref=a.at[:, pl.ds(2 * peer, 2)], dst_ref=recv_r.at[r],
            send_sem=send_b.at[d], recv_sem=recv_b.at[d],
            device_id={"row": peer}, device_id_type=MESH,
        )

    for part in range(CHUNKS):
        loop(1, cols, lambda d: to_col(part, d).start())
    loop(1, rows, lambda d: to_row(d).start())

    y_right = {"col": x * ny + lax.rem(y + 1, ny)}
    y_left = {"col": x * ny + lax.rem(y + ny - 1, ny)}
    partner = {"row": 2 * z + 1 - core}
    rings, copies = [], []

    def ring_y(*views):
        rings.append(Ring(sems, ny, y, views, y_right, y_left))
        return rings[-1]

    def hops_y(*views):
        rings.append(Hops(sems, ny, y, views, lambda i: {"col": x * ny + i}))
        return rings[-1]

    def hops_z(*views):
        rings.append(Hops(sems, nz, z, views, lambda i: {"row": 2 * i + core}))
        return rings[-1]

    def send(src, dst, device):
        copy = sems.copy(src, dst, device, sems.take())
        copy.start()
        copies.append(copy)
        return copy

    def spread_x(ref):
        return [
            send(ref, ref, {"col": lax.rem(x + d, nx) * ny + y}) for d in range(1, nx)
        ]

    forwards = []

    def forward(ref):
        forwards.append(send(ref, ref, partner))

    def x_then_y(gather_y, view, first, step, arrived):
        copies = spread_x(view(x, y))
        yield first
        for copy in copies:
            copy.wait_recv()
        arrived(y)
        yield from gather_y(*[lambda i, k=k: view(k, i) for k in range(nx)]).run(step, arrived)

    def y_then_x(gather_y, view, first, spread, arrived):
        pending = []

        def have(i):
            pending.append((i, spread_x(view(x, i))))

        have(y)
        yield from gather_y(lambda i: view(x, i)).run(first, have)
        for i, copies in pending:
            yield spread
            for copy in copies:
                copy.wait_recv()
            arrived(i)

    def cross_chain(part):
        swap = send(
            xbuf.at[:, :, :, span(part)], zbuf.at[z, pl.ds(2 * core, 2), :, :, span(part)], partner
        )
        yield TIMES["swap"]
        swap.wait_recv()
        yield from hops_z(
            *[lambda i, k=k: zbuf.at[i, pl.ds(2 * k, 2), :, :, span(part)] for k in range(2)]
        ).run(TIMES["z"])
        for h in range(half):
            m = core * half + h
            for j in range(panels - 1):
                p = pivots[j + (j >= m).astype(jnp.int32)]
                ppg[m, x, y, j, :, span(part)] = zbuf[p // 4, lax.rem(p, 4), h, :, span(part)]
        for h, order in ((0, x_then_y), (1, y_then_x)):
            m = core * half + h

            def view(i, j, m=m):
                return ppg.at[m, i, j, :, :, span(part)]

            def arrived(i, view=view):
                forward(view(slice(None), i))

            yield (0, order(hops_y, view, *TIMES["pp"][h], arrived))

    def column_chain(part):
        loop(1, cols, lambda d: to_col(part, d).wait_recv())
        for h in range(half):
            theirs = recv_c[pivots[(1 - core) * half + h], :, :, span(part)]
            mine = recv_c[pivots[core * half + h], :, :, span(part)]
            for b in range(2):
                xbuf[b, h, :, span(part)] = theirs[b]
                zbuf[z, 2 * core + b, h, :, span(part)] = mine[b]
        for m in range(panels):
            piece = recv_c[pivots[m], :, :, span(part)]
            for b in range(2):
                colg[b, x, y, m, :, span(part)] = piece[b]
        yield (0, cross_chain(part))
        for b, order in ((0, x_then_y), (1, y_then_x)):

            def view(i, j, b=b):
                return colg.at[b, i, j, :, :, span(part)]

            yield (0, order((ring_y, hops_y)[b], view, *TIMES["col"][b], lambda i: None))

    def partner_swap(ref):
        copy = send(ref, ref, partner)
        yield TIMES["share"]
        copy.wait_recv()

    def inverse_chain():
        yield 0
        yield from hops_z(lambda i: invg.at[i, core]).run(TIMES["inv"])
        yield from partner_swap(invg.at[:, core])

    def row_chain():
        loop(1, rows, lambda d: to_row(d).wait_recv())
        for k in range(panels):
            p = pivots[k]
            rowg[z, core, k] = recv_r[p // 2, lax.rem(p, 2)]
        yield from hops_z(lambda i: rowg.at[i, core]).run(TIMES["row"])
        yield from partner_swap(rowg.at[:, core])

    interleave(
        [(TIMES["a2a"][part], column_chain(part)) for part in range(CHUNKS)]
        + [(TIMES["rows"], row_chain()), (23.0, inverse_chain())]
    )
    for copy in forwards:
        copy.wait_recv()
    for ring in rings:
        ring.drain()
    for copy in copies:
        copy.wait_send()
    for part in range(CHUNKS):
        loop(1, cols, lambda d: to_col(part, d).wait_send())
    loop(1, rows, lambda d: to_row(d).wait_send())


def halves(value):
    high = value.astype(BF16)
    return high, (value - high.astype(F32)).astype(BF16)


def product(left, right):
    (lh, ll), (rh, rl) = left, right
    dot = functools.partial(jnp.dot, preferred_element_type=F32)
    return dot(lh, rh) + (dot(lh, rl) + dot(ll, rh))


def eliminate(panels, width, pivots, row_mask, col_mask, a, colg, ppg, rowg, invg, out, xh, xl, keep):
    my_col = lax.axis_index("col")
    my_rows = [lax.axis_index("row") * 2 + b for b in range(2)]
    square = (width, width)

    def whole(ref, *index):
        return ref[index].reshape(square)

    def left_of(i, step):
        if i < 2:
            return whole(colg, i, slice(None), slice(None), step)
        return whole(ppg, step, slice(None), slice(None), i - 2 - (i - 2 > step))

    def done(block, step):
        hit = block == pivots[0]
        for k in range(1, step + 1):
            hit = hit | (block == pivots[k])
        return hit

    for step in range(panels):
        inverse = halves(whole(invg, slice(None), slice(None), step))
        later = range(step + 1, panels)
        factors = [jnp.where(done(i, step), 0.0, row_mask[step, i].astype(F32)) for i in my_rows]
        factors += [row_mask[step, pivots[k]].astype(F32) for k in later]
        places = [0, 1] + [2 + k for k in later]
        for n, (i, factor) in enumerate(zip(places, factors)):
            high, low = halves(left_of(i, step) * factor)
            xh[n] = high
            xl[n] = low
        for j in later:
            solved = product(inverse, halves(left_of(2 + step, j)))
            right = halves(solved * col_mask[step, pivots[j]].astype(F32))
            for n, i in enumerate(places):
                if i - 2 == j:
                    continue
                change = product((xh[n], xl[n]), right)
                if i < 2:
                    shape = colg.shape[1:3] + colg.shape[4:]
                    colg[i, :, :, j] -= change.reshape(shape)
                else:
                    shape = ppg.shape[1:3] + ppg.shape[4:]
                    ppg[j, :, :, i - 2 - (i - 2 > j)] -= change.reshape(shape)
        solved = product(inverse, halves(whole(rowg, slice(None), slice(None), step)))
        keep[step] = solved
        factor = jnp.where(done(my_col, step), 0.0, col_mask[step, my_col].astype(F32))
        right = halves(solved * factor)
        for n, i in enumerate(places):
            change = product((xh[n], xl[n]), right)
            if i < 2:
                span = pl.ds(i * width, width)
                before = whole(a, i) if step == 0 else out[span, :]
                out[span, :] = before - change
            else:
                shape = rowg.shape[:2] + rowg.shape[3:]
                rowg[:, :, i - 2] -= change.reshape(shape)

    for b in range(2):
        span = pl.ds(b * width, width)
        value = out[span, :]
        for k in range(panels):
            mine = my_rows[b] == pivots[k]
            if k == 0:
                pivot_row = keep[k]
            else:
                pivot_row = jnp.where(done(my_col, k - 1), whole(rowg, slice(None), slice(None), k), keep[k])
            value = jnp.where(mine, pivot_row, value)
        out[span, :] = value


def on_device(nz, nx, ny, matrix, inverses, pivots, row_mask, col_mask):
    panels, _, width = inverses.shape
    rows, cols = 2 * nz, nx * ny
    part = width // cols
    blocks = matrix.reshape(2, cols, part, width)
    slices = inverses.reshape(panels, 2, part, width)
    vmem = pl.BlockSpec(memory_space=pltpu.VMEM)
    smem = pl.BlockSpec(memory_space=pltpu.SMEM)
    half = panels // 2
    count = 320
    return pl.pallas_call(
        functools.partial(kernel, nz, nx, ny, panels, width),
        out_shape=jax.ShapeDtypeStruct((2 * width, width), F32),
        in_specs=[smem, smem, smem, vmem, vmem],
        out_specs=vmem,
        scratch_shapes=[
            pltpu.VMEM((2, nx, ny, panels, part, width), F32),
            pltpu.VMEM((panels, nx, ny, panels - 1, part, width), F32),
            pltpu.VMEM((nz, 2, panels, 2, part, width), F32),
            pltpu.VMEM((nz, 2, panels, 2, part, width), F32),
            pltpu.VMEM((1 + panels, width, width), BF16),
            pltpu.VMEM((1 + panels, width, width), BF16),
            pltpu.VMEM((panels, width, width), F32),
            pltpu.VMEM((cols, 2, part, width), F32),
            pltpu.VMEM((rows, 2, 2, part, width), F32),
            pltpu.VMEM((nz, 4, half, part, width), F32),
            pltpu.VMEM((2, half, part, width), F32),
            pltpu.SemaphoreType.DMA((CHUNKS, cols)),
            pltpu.SemaphoreType.DMA((CHUNKS, cols)),
            pltpu.SemaphoreType.DMA((rows,)),
            pltpu.SemaphoreType.DMA((rows,)),
            pltpu.SemaphoreType.DMA((count,)),
            pltpu.SemaphoreType.DMA((count,)),
        ],
        compiler_params=pltpu.CompilerParams(collective_id=0, has_side_effects=True),
    )(pivots, row_mask, col_mask, blocks, slices)


def kernel(
    nz, nx, ny, panels, width, pivots, row_mask, col_mask, a, inv, out,
    colg, ppg, rowg, invg, xh, xl, keep, *scratch,
):
    gather(nz, nx, ny, panels, pivots, a, inv, colg, ppg, rowg, invg, *scratch)
    eliminate(panels, width, pivots, row_mask, col_mask, a, colg, ppg, rowg, invg, out, xh, xl, keep)


def solution(mesh):
    rows, cols = mesh.shape["row"], mesh.shape["col"]
    nx = 4 if cols == 32 else 2
    in_specs = (P("row", "col"), P(None, "row", None), P(), P(), P())
    return jax.shard_map(
        functools.partial(on_device, rows // 2, nx, cols // nx),
        mesh=mesh, in_specs=in_specs, out_specs=P("row", "col"), check_vma=False,
    )
```

```python
import functools

import jax
import jax.numpy as jnp
from jax import lax
from jax.experimental import pallas as pl
from jax.experimental.pallas import tpu as pltpu
from jax.sharding import PartitionSpec as P

MESH = pl.DeviceIdType.MESH
F32 = jnp.float32
BF16 = jnp.bfloat16
CHUNKS = 1
SPLIT = 1
TIMES = {
    "a2a": (10.0,), "rows": 24.0, "swap": 2.5, "z": 5.0, "inv": 8.0, "row": 8.0, "share": 3.0,
    "col": ((5.0, 4.5), (5.0, 1.2)), "pp": ((3.5, 6.0), (4.0, 0.6)),
}


class Sems:
    def __init__(self, send, recv):
        self.send, self.recv, self.used = send, recv, 0

    def take(self, count=1):
        first = self.used
        self.used += count
        return first

    def copy(self, src, dst, device, index):
        return pltpu.make_async_remote_copy(
            src_ref=src,
            dst_ref=dst,
            send_sem=self.send.at[index],
            recv_sem=self.recv.at[index],
            device_id=device,
            device_id_type=MESH,
        )


class Ring:
    def __init__(self, sems, n, me, views, right, left):
        self.n, self.me, self.steps = n, me, n // 2
        self.pieces = []
        for view in views:
            ways = []
            for s in range(self.steps):
                slot = lax.rem(me - s + n, n)
                ways.append([sems.copy(view(slot), view(slot), right, sems.take())])
                if s < n - 1 - self.steps:
                    slot = lax.rem(me + s, n)
                    ways[-1].append(sems.copy(view(slot), view(slot), left, sems.take()))
            self.pieces.append(ways)

    def run(self, delay, arrived=None):
        for s in range(self.steps + 1):
            for n, ways in enumerate(self.pieces):
                if s > 0:
                    yield 0.3 if n else delay
                    for copy in ways[s - 1]:
                        copy.wait_recv()
                if s < self.steps:
                    for copy in ways[s]:
                        copy.start()
            if s > 0 and arrived is not None:
                arrived(lax.rem(self.me - s + self.n, self.n))
                if s < self.n - self.steps:
                    arrived(lax.rem(self.me + s, self.n))

    def drain(self):
        for ways in self.pieces:
            for step in ways:
                for copy in step:
                    copy.wait_send()


class Hops:
    def __init__(self, sems, n, me, views, at):
        self.n, self.me, self.all = n, me, []
        self.first, self.second = [], []

        def copy(view, slot, to):
            slot = lax.rem(me + slot + n, n)
            made = sems.copy(view(slot), view(slot), at(lax.rem(me + to + n, n)), sems.take())
            self.all.append(made)
            return made

        for p, view in enumerate(views):
            if n < 6:
                self.first.append([copy(view, 0, d) for d in range(1, n)])
                self.second.append([])
            else:
                self.first.append([copy(view, 0, d) for d in (2, -2, 1, -1)])
                far = 2 if p % 2 == 0 else -2
                self.second.append([copy(view, -2, 1), copy(view, 2, -1), copy(view, -far, far)])

    def slot(self, d):
        return lax.rem(self.me + d + self.n, self.n)

    def run(self, delay, arrived=None):
        for copies in self.first:
            for copy in copies:
                copy.start()
        for n, copies in enumerate(self.first):
            yield 0.3 if n else delay
            for copy in copies[:2]:
                copy.wait_recv()
            for copy in self.second[n]:
                copy.start()
        for copies in self.first:
            for copy in copies[2:]:
                copy.wait_recv()
        near = [-d for d in range(1, self.n)] if self.n < 6 else [-1, 1, -2, 2]
        if arrived is not None:
            for d in near:
                arrived(self.slot(d))
        if self.n >= 6:
            for n, copies in enumerate(self.second):
                yield 0.3 if n else delay
                for copy in copies:
                    copy.wait_recv()
            if arrived is not None:
                for d in (-3, 3, 4):
                    arrived(self.slot(d))

    def drain(self):
        for copy in self.all:
            copy.wait_send()


def interleave(chains):
    queue = [(start, n, chain) for n, (start, chain) in enumerate(chains)]
    count = len(queue)
    while queue:
        now, n, chain = min(queue, key=lambda item: item[:2])
        queue.remove((now, n, chain))
        for event in chain:
            if isinstance(event, tuple):
                queue.append((now + event[0], count, event[1]))
                count += 1
            else:
                queue.append((now + event, n, chain))
                break


def gather(
    nz, nx, ny, panels, pivots, a_in, a, load_sem, inv, colg, ppg, rowg, invg,
    recv_c, recv_r, zbuf, xbuf, send_a, recv_a, send_b, recv_b, send_s, recv_s,
):
    rows, cols = 2 * nz, nx * ny
    half = panels // 2
    r, c = lax.axis_index("row"), lax.axis_index("col")
    z, core = r // 2, lax.rem(r, 2)
    x, y = c // ny, lax.rem(c, ny)
    lanes = colg.shape[-1] // CHUNKS

    barrier = pltpu.get_barrier_semaphore()

    def loop(low, high, act):
        def body(d, carry):
            act(d)
            return carry
        lax.fori_loop(low, high, body, 0)

    def greet(axis, me, n):
        loop(1, n, lambda d: pl.semaphore_signal(
            barrier, inc=1, device_id={axis: lax.rem(me + d, n)}, device_id_type=MESH
        ))

    load = pltpu.make_async_copy(a_in, a, load_sem)
    load.start()
    greet("col", c, cols)
    greet("row", r, rows)
    load.wait()
    recv_c[c] = a[:, c]
    recv_r[r] = a[:, pl.ds(2 * r, 2)]
    invg[z, core] = inv[...]
    pl.semaphore_wait(barrier, cols + rows - 2)

    sems = Sems(send_s, recv_s)

    def span(part):
        return pl.ds(part * lanes, lanes)

    def to_col(part, d):
        peer = lax.rem(c + d, cols)
        return pltpu.make_async_remote_copy(
            src_ref=a.at[:, peer, :, span(part)], dst_ref=recv_c.at[c, :, :, span(part)],
            send_sem=send_a.at[part, d], recv_sem=recv_a.at[part, d],
            device_id={"col": peer}, device_id_type=MESH,
        )

    def to_row(d):
        peer = lax.rem(r + d, rows)
        return pltpu.make_async_remote_copy(
            src_ref=a.at[:, pl.ds(2 * peer, 2)], dst_ref=recv_r.at[r],
            send_sem=send_b.at[d], recv_sem=recv_b.at[d],
            device_id={"row": peer}, device_id_type=MESH,
        )

    for part in range(CHUNKS):
        loop(1, cols, lambda d: to_col(part, d).start())
    loop(1, rows, lambda d: to_row(d).start())

    y_right = {"col": x * ny + lax.rem(y + 1, ny)}
    y_left = {"col": x * ny + lax.rem(y + ny - 1, ny)}
    partner = {"row": 2 * z + 1 - core}
    rings, copies = [], []

    def ring_y(*views):
        rings.append(Ring(sems, ny, y, views, y_right, y_left))
        return rings[-1]

    def hops_y(*views):
        rings.append(Hops(sems, ny, y, views, lambda i: {"col": x * ny + i}))
        return rings[-1]

    def hops_z(*views):
        rings.append(Hops(sems, nz, z, views, lambda i: {"row": 2 * i + core}))
        return rings[-1]

    def send(src, dst, device):
        copy = sems.copy(src, dst, device, sems.take())
        copy.start()
        copies.append(copy)
        return copy

    def spread_x(ref):
        return [
            send(ref, ref, {"col": lax.rem(x + d, nx) * ny + y}) for d in range(1, nx)
        ]

    forwards = []

    def forward(ref):
        forwards.append(send(ref, ref, partner))

    def x_then_y(gather_y, view, first, step, arrived):
        copies = spread_x(view(x, y))
        yield first
        for copy in copies:
            copy.wait_recv()
        arrived(y)
        yield from gather_y(*[lambda i, k=k: view(k, i) for k in range(nx)]).run(step, arrived)

    def y_then_x(gather_y, view, first, spread, arrived):
        pending = []

        def have(i):
            pending.append((i, spread_x(view(x, i))))

        have(y)
        yield from gather_y(lambda i: view(x, i)).run(first, have)
        for i, copies in pending:
            yield spread
            for copy in copies:
                copy.wait_recv()
            arrived(i)

    def cross_chain(part):
        swap = send(
            xbuf.at[:, :, :, span(part)], zbuf.at[z, pl.ds(2 * core, 2), :, :, span(part)], partner
        )
        yield TIMES["swap"]
        swap.wait_recv()
        yield from hops_z(
            *[lambda i, k=k: zbuf.at[i, pl.ds(2 * k, 2), :, :, span(part)] for k in range(2)]
        ).run(TIMES["z"])
        for h in range(half):
            m = core * half + h
            for j in range(panels - 1):
                p = pivots[j + (j >= m).astype(jnp.int32)]
                ppg[core, x, y, h * (panels - 1) + j, :, span(part)] = zbuf[
                    p // 4, lax.rem(p, 4), h, :, span(part)
                ]
        whole = half * (panels - 1)
        for h, order in ((0, x_then_y), (1, y_then_x)):
            some = pl.ds(0, SPLIT) if h == 0 else pl.ds(SPLIT, whole - SPLIT)

            def view(i, j, some=some):
                return ppg.at[core, i, j, some, :, span(part)]

            def arrived(i, view=view):
                forward(view(slice(None), i))

            yield (0, order(hops_y, view, *TIMES["pp"][h], arrived))

    def column_chain(part):
        loop(1, cols, lambda d: to_col(part, d).wait_recv())
        for h in range(half):
            theirs = recv_c[pivots[(1 - core) * half + h], :, :, span(part)]
            mine = recv_c[pivots[core * half + h], :, :, span(part)]
            for b in range(2):
                xbuf[b, h, :, span(part)] = theirs[b]
                zbuf[z, 2 * core + b, h, :, span(part)] = mine[b]
        for m in range(panels):
            piece = recv_c[pivots[m], :, :, span(part)]
            for b in range(2):
                colg[b, x, y, m, :, span(part)] = piece[b]
        yield (0, cross_chain(part))
        for b, order in ((0, x_then_y), (1, y_then_x)):

            def view(i, j, b=b):
                return colg.at[b, i, j, :, :, span(part)]

            yield (0, order((ring_y, hops_y)[b], view, *TIMES["col"][b], lambda i: None))

    def partner_swap(ref):
        copy = send(ref, ref, partner)
        yield TIMES["share"]
        copy.wait_recv()

    def inverse_chain():
        yield 0
        yield from hops_z(lambda i: invg.at[i, core]).run(TIMES["inv"])
        yield from partner_swap(invg.at[:, core])

    def row_chain():
        loop(1, rows, lambda d: to_row(d).wait_recv())
        for k in range(panels):
            p = pivots[k]
            rowg[z, core, k] = recv_r[p // 2, lax.rem(p, 2)]
        yield from hops_z(lambda i: rowg.at[i, core]).run(TIMES["row"])
        yield from partner_swap(rowg.at[:, core])

    interleave(
        [(TIMES["a2a"][part], column_chain(part)) for part in range(CHUNKS)]
        + [(TIMES["rows"], row_chain()), (23.0, inverse_chain())]
    )
    for copy in forwards:
        copy.wait_recv()
    for ring in rings:
        ring.drain()
    for copy in copies:
        copy.wait_send()
    for part in range(CHUNKS):
        loop(1, cols, lambda d: to_col(part, d).wait_send())
    loop(1, rows, lambda d: to_row(d).wait_send())


def halves(value):
    high = value.astype(BF16)
    return high, (value - high.astype(F32)).astype(BF16)


def product(left, right):
    (lh, ll), (rh, rl) = left, right
    dot = functools.partial(jnp.dot, preferred_element_type=F32)
    return dot(lh, rh) + (dot(lh, rl) + dot(ll, rh))


def eliminate(panels, width, pivots, row_mask, col_mask, a, colg, ppg, rowg, invg, out, xh, xl, keep):
    my_col = lax.axis_index("col")
    my_rows = [lax.axis_index("row") * 2 + b for b in range(2)]
    square = (width, width)

    def whole(ref, *index):
        return ref[index].reshape(square)

    def crossing(k, m):
        half = panels // 2
        return m // half, slice(None), slice(None), m % half * (panels - 1) + k - (k > m)

    def left_of(i, step):
        if i < 2:
            return whole(colg, i, slice(None), slice(None), step)
        return whole(ppg, *crossing(i - 2, step))

    def done(block, step):
        hit = block == pivots[0]
        for k in range(1, step + 1):
            hit = hit | (block == pivots[k])
        return hit

    for step in range(panels):
        inverse = halves(whole(invg, slice(None), slice(None), step))
        later = range(step + 1, panels)
        factors = [jnp.where(done(i, step), 0.0, row_mask[step, i].astype(F32)) for i in my_rows]
        factors += [row_mask[step, pivots[k]].astype(F32) for k in later]
        places = [0, 1] + [2 + k for k in later]
        for n, (i, factor) in enumerate(zip(places, factors)):
            high, low = halves(left_of(i, step) * factor)
            xh[n] = high
            xl[n] = low
        for j in later:
            solved = product(inverse, halves(left_of(2 + step, j)))
            right = halves(solved * col_mask[step, pivots[j]].astype(F32))
            for n, i in enumerate(places):
                if i - 2 == j:
                    continue
                change = product((xh[n], xl[n]), right)
                if i < 2:
                    shape = colg.shape[1:3] + colg.shape[4:]
                    colg[i, :, :, j] -= change.reshape(shape)
                else:
                    shape = ppg.shape[1:3] + ppg.shape[4:]
                    ppg[crossing(i - 2, j)] -= change.reshape(shape)
        solved = product(inverse, halves(whole(rowg, slice(None), slice(None), step)))
        keep[step] = solved
        factor = jnp.where(done(my_col, step), 0.0, col_mask[step, my_col].astype(F32))
        right = halves(solved * factor)
        for n, i in enumerate(places):
            change = product((xh[n], xl[n]), right)
            if i < 2:
                span = pl.ds(i * width, width)
                before = whole(a, i) if step == 0 else out[span, :]
                out[span, :] = before - change
            else:
                shape = rowg.shape[:2] + rowg.shape[3:]
                rowg[:, :, i - 2] -= change.reshape(shape)

    for b in range(2):
        span = pl.ds(b * width, width)
        value = out[span, :]
        for k in range(panels):
            mine = my_rows[b] == pivots[k]
            if k == 0:
                pivot_row = keep[k]
            else:
                pivot_row = jnp.where(done(my_col, k - 1), whole(rowg, slice(None), slice(None), k), keep[k])
            value = jnp.where(mine, pivot_row, value)
        out[span, :] = value


def on_device(nz, nx, ny, matrix, inverses, pivots, row_mask, col_mask):
    panels, _, width = inverses.shape
    rows, cols = 2 * nz, nx * ny
    part = width // cols
    blocks = matrix.reshape(2, cols, part, width)
    slices = inverses.reshape(panels, 2, part, width)
    vmem = pl.BlockSpec(memory_space=pltpu.VMEM)
    smem = pl.BlockSpec(memory_space=pltpu.SMEM)
    half = panels // 2
    count = 320
    return pl.pallas_call(
        functools.partial(kernel, nz, nx, ny, panels, width),
        out_shape=jax.ShapeDtypeStruct((2 * width, width), F32),
        in_specs=[smem, smem, smem, pl.BlockSpec(memory_space=pl.ANY), vmem],
        out_specs=vmem,
        scratch_shapes=[
            pltpu.VMEM((2, cols, part, width), F32),
            pltpu.SemaphoreType.DMA,
            pltpu.VMEM((2, nx, ny, panels, part, width), F32),
            pltpu.VMEM((2, nx, ny, half * (panels - 1), part, width), F32),
            pltpu.VMEM((nz, 2, panels, 2, part, width), F32),
            pltpu.VMEM((nz, 2, panels, 2, part, width), F32),
            pltpu.VMEM((1 + panels, width, width), BF16),
            pltpu.VMEM((1 + panels, width, width), BF16),
            pltpu.VMEM((panels, width, width), F32),
            pltpu.VMEM((cols, 2, part, width), F32),
            pltpu.VMEM((rows, 2, 2, part, width), F32),
            pltpu.VMEM((nz, 4, half, part, width), F32),
            pltpu.VMEM((2, half, part, width), F32),
            pltpu.SemaphoreType.DMA((CHUNKS, cols)),
            pltpu.SemaphoreType.DMA((CHUNKS, cols)),
            pltpu.SemaphoreType.DMA((rows,)),
            pltpu.SemaphoreType.DMA((rows,)),
            pltpu.SemaphoreType.DMA((count,)),
            pltpu.SemaphoreType.DMA((count,)),
        ],
        compiler_params=pltpu.CompilerParams(collective_id=0, has_side_effects=True),
    )(pivots, row_mask, col_mask, blocks, slices)


def kernel(
    nz, nx, ny, panels, width, pivots, row_mask, col_mask, a_in, inv, out,
    a, load_sem, colg, ppg, rowg, invg, xh, xl, keep, *scratch,
):
    gather(nz, nx, ny, panels, pivots, a_in, a, load_sem, inv, colg, ppg, rowg, invg, *scratch)
    eliminate(panels, width, pivots, row_mask, col_mask, a, colg, ppg, rowg, invg, out, xh, xl, keep)


def solution(mesh):
    rows, cols = mesh.shape["row"], mesh.shape["col"]
    nx = 4 if cols == 32 else 2
    in_specs = (P("row", "col"), P(None, "row", None), P(), P(), P())
    return jax.shard_map(
        functools.partial(on_device, rows // 2, nx, cols // nx),
        mesh=mesh, in_specs=in_specs, out_specs=P("row", "col"), check_vma=False,
    )
```
